32 devices in a mesh: row: 8 (over y, x, core), col: 4 (over z).
Axes of the slice: x: 2, y: 2, z: 4, core: 2. Of those that a mesh axis runs over, the one named last changes fastest.
Arguments:
- base_weights: bfloat16 [2, 8192, 28672], P(None, 'row', 'col'), may hold values from -6 to 6
- left_factors: bfloat16 [2, 8192, 4, 128], P(None, 'row', 'col'), may hold values from -6 to 6
- right_factors: bfloat16 [2, 4, 128, 28672], P(None, 'col', None, 'row'), may hold values from -6 to 6
- client_adapter_ranks: int32 [4], replicated, may hold values from 16 to 128, as said below
- step_counts: int32 [4], replicated, may hold values from 100 to 1000
- worker_slot: int32 [4], replicated, may hold values from 0 to 3, each once
Outputs:
- merged: bfloat16 [2, 8192, 28672], P(None, 'row', 'col')
The draws below stay inside these ranges and needn't reach their ends.
Inputs may be any that keep to these rules, and one draw needn't show every extreme that they name: `client_adapter_ranks`: each rank is a multiple of 16; the ranks sum to 256; at least one rank equals 128. `worker_slot`: a permutation: every slot holds exactly one worker's factors.
All inputs are finite; a program needn't handle non-finite values.
Results may differ from the reference program's by a relative error of at most 0.0045.
Values may be sent and summed in bfloat16 or wider, within the bound.
No kernel may reach another device: no remote copies, remote signals or barrier semaphores. Data moves between devices by JAX's collectives and lax.ppermute only.
A program may use at most 192 MiB of HBM per device.

```python
import jax
import jax.numpy as jnp
from jax import lax

D = 8192
FF = 28672
RMAX = 128
PROJ = 2
ADAPTER_ALPHA = 32
CLIENT_COUNT = 4
RANKS = 256


def draw_client_adapter_ranks(key, part):
    key_big, key_fill = jax.random.split(jax.random.fold_in(key, 17))
    worker_ids = jnp.arange(CLIENT_COUNT, dtype=jnp.int32)
    big_slot = jax.random.randint(key_big, (), 0, CLIENT_COUNT)
    rank_units = jnp.where(worker_ids == big_slot, 8, 1).astype(jnp.int32)
    fill_keys = jax.random.split(key_fill, 3 * CLIENT_COUNT - 7)

    def increment_unit(current, subkey):
        scores = jax.random.randint(subkey, (CLIENT_COUNT,), 0, 1 << 20) * CLIENT_COUNT + worker_ids
        scores = jnp.where(current < 8, scores, -1)
        selected_rank = jnp.argmax(scores)
        return (current + (worker_ids == selected_rank).astype(jnp.int32), None)
    rank_units, unused = lax.scan(increment_unit, rank_units, fill_keys)
    return (rank_units * (RMAX // 8)).astype(jnp.int32)


def plant(values, rng, smallest, largest):
    index_at = [jax.random.randint(jax.random.fold_in(rng, axis), (), 0, length) for axis, length in enumerate(values.shape)]
    widest = values.shape.index(max(values.shape))
    next_to = index_at[:widest] + [(index_at[widest] + 1) % values.shape[widest]] + index_at[widest + 1:]
    return values.at[tuple(index_at)].set(smallest).at[tuple(next_to)].set(largest)


def block_scale(stream_key, dims, shards, least, high):
    def one(dim, blocks):
        steps = jax.random.uniform(jax.random.fold_in(jax.random.fold_in(stream_key, 6), dim), (blocks,), jnp.float32, least / len(shards), high / len(shards))
        return jnp.repeat(jnp.exp(steps), dims[dim] // blocks).reshape((-1,) + (1,) * (len(dims) - dim - 1))

    gain = one(*shards[0])
    for cut in shards[1:]:
        gain = gain * one(*cut)
    return gain


def scatter_about(key, extent, scale, reach, pieces=(), kind=jnp.bfloat16):
    drawn = jax.random.normal(key, extent, jnp.float32) * scale
    if len(pieces) > 0:
        drawn = block_scale(key, extent, pieces, -0.22, 0.18) * drawn
    return jnp.clip(drawn, min=-reach, max=reach).astype(kind)


def setup_inputs(seed: int = 0) -> dict:
    key_of = jax.random.split(jax.random.key(seed), 7)
    return {
        "base_weights": scatter_about(key_of[0], (PROJ, D, FF), 1.0, 6.0, ((1, 8), (2, 4))),
        "left_factors": scatter_about(key_of[1], (PROJ, D, CLIENT_COUNT, RMAX), 1.0, 6.0, ((1, 8), (2, 4))),
        "right_factors": scatter_about(key_of[2], (PROJ, CLIENT_COUNT, RMAX, FF), 1.0, 6.0, ((1, 4), (3, 8))),
        "client_adapter_ranks": draw_client_adapter_ranks(jax.random.fold_in(key_of[6], 71), 0),
        "step_counts": plant(jax.random.randint(key_of[4], (CLIENT_COUNT,), 100, 1001), jax.random.fold_in(key_of[4], 1), 100, 1000).astype(jnp.int32),
        "worker_slot": jax.random.permutation(key_of[5], CLIENT_COUNT).astype(jnp.int32),
    }


def slot_tables(client_adapter_ranks, step_counts, worker_slot):
    slot_ids = jnp.arange(CLIENT_COUNT, dtype=jnp.int32)
    slot_hot = worker_slot[:, None] == slot_ids[None, :]
    rank_slot = jnp.sum(jnp.where(slot_hot, client_adapter_ranks[:, None], 0), axis=0).astype(jnp.int32)
    counts = step_counts.astype(jnp.float32)
    per_step_portion = counts / jnp.sum(counts)
    client_scale = ADAPTER_ALPHA * per_step_portion / client_adapter_ranks.astype(jnp.float32)
    slot_scale_factor = jnp.sum(jnp.where(slot_hot, client_scale[:, None], 0.0), axis=0)
    return rank_slot, slot_scale_factor


def packed_index(rank_slot, rank_cap, total):
    workers = rank_slot.shape[0]
    slot_ends = jnp.cumsum(rank_slot).astype(jnp.int32)
    slot_starts = slot_ends - rank_slot
    position = jnp.arange(total, dtype=jnp.int32)
    slot_of = jnp.sum((position[:, None] >= slot_ends[None, :]).astype(jnp.int32), axis=1)
    slot_ids = jnp.arange(workers, dtype=jnp.int32)
    start_of = jnp.sum(jnp.where(slot_of[:, None] == slot_ids[None, :], slot_starts[None, :], 0), axis=1)
    return (slot_of * rank_cap + position - start_of).astype(jnp.int32)


def reference(base_weights, left_factors, right_factors, client_adapter_ranks, step_counts, worker_slot):
    rank_slot, slot_scale_factor = slot_tables(client_adapter_ranks, step_counts, worker_slot)
    columns = jnp.arange(RMAX, dtype=jnp.int32)
    rank_scale = jnp.where(columns[None, :] < rank_slot[:, None], slot_scale_factor[:, None], 0.0)
    scaled_right = (right_factors.astype(jnp.float32) * rank_scale[None, :, :, None]).astype(jnp.bfloat16)
    flat_index = packed_index(rank_slot, RMAX, RANKS)

    def merge_one(operands):
        base_tile, left_block, right_block = operands
        left_pack = jnp.take(left_block.reshape(D, CLIENT_COUNT * RMAX), flat_index, axis=1)
        right_pack = jnp.take(right_block.reshape(CLIENT_COUNT * RMAX, FF), flat_index, axis=0)
        delta_tile = jnp.dot(left_pack.astype(jnp.float32), right_pack.astype(jnp.float32), preferred_element_type=jnp.float32)
        return (base_tile.astype(jnp.float32) + delta_tile).astype(jnp.bfloat16)

    return lax.map(merge_one, (base_weights, left_factors, scaled_right))
```

```python
import jax
import jax.numpy as jnp
from jax import lax
from jax.experimental import pallas as pl
from jax.experimental.pallas import tpu as pltpu
from jax.sharding import PartitionSpec as P

ADAPTER_ALPHA = 32
LANES = 128
RANK_STEP = 16


def slot_tables(client_adapter_ranks, step_counts, worker_slot):
    workers = client_adapter_ranks.shape[0]
    slot_ids = jnp.arange(workers, dtype=jnp.int32)
    slot_hot = worker_slot[:, None] == slot_ids[None, :]
    rank_slot = jnp.sum(jnp.where(slot_hot, client_adapter_ranks[:, None], 0), axis=0)
    counts = step_counts.astype(jnp.float32)
    per_step_portion = counts / jnp.sum(counts)
    client_scale = ADAPTER_ALPHA * per_step_portion / client_adapter_ranks.astype(jnp.float32)
    slot_scale_factor = jnp.sum(jnp.where(slot_hot, client_scale[:, None], 0.0), axis=0)
    return (rank_slot, slot_scale_factor)


def merge_tile(base_tile, left_piece, right_piece):
    tile_rows = base_tile.shape[0]
    rank_cap = right_piece.shape[1]
    block_width = right_piece.shape[2]
    row_count = lax.axis_size("row")
    col_count = lax.axis_size("col")
    row_ratio = row_count // col_count
    left_all = lax.all_gather(left_piece, "col", axis=1, tiled=True)
    sub_width = block_width // row_count
    split_view = right_piece.reshape(1, rank_cap, row_count, sub_width)
    spread = lax.all_to_all(split_view, "row", split_axis=2, concat_axis=2, tiled=True)
    pair_view = spread.reshape(1, rank_cap, col_count, row_ratio, sub_width)
    slot_pieces = lax.all_to_all(pair_view, "col", split_axis=2, concat_axis=0, tiled=True)
    join_view = slot_pieces.reshape(col_count, rank_cap, row_ratio, 1, sub_width)
    joined = lax.all_gather(join_view, "row", axis=3, tiled=True)
    right_cols = joined.reshape(col_count, rank_cap, row_ratio * block_width)
    left_flat = left_all.reshape(tile_rows, -1)
    right_flat = right_cols.reshape(left_flat.shape[1], -1)
    delta_tile = jnp.dot(left_flat, right_flat, preferred_element_type=jnp.float32)
    return (base_tile.astype(jnp.float32) + delta_tile).astype(jnp.bfloat16)


def plain_body(base_weights, left_factors, right_factors, client_adapter_ranks, step_counts, worker_slot):
    workers = client_adapter_ranks.shape[0]
    rank_cap = right_factors.shape[2]
    rank_slot, slot_scale_factor = slot_tables(client_adapter_ranks, step_counts, worker_slot)
    own_hot = jnp.arange(workers, dtype=jnp.int32) == lax.axis_index("col")
    own_rank = jnp.sum(jnp.where(own_hot, rank_slot, 0))
    own_scale = jnp.sum(jnp.where(own_hot, slot_scale_factor, 0.0))
    rank_scale = jnp.where(jnp.arange(rank_cap, dtype=jnp.int32) < own_rank, own_scale, 0.0)
    scaled_right = (right_factors.astype(jnp.float32) * rank_scale[None, None, :, None]).astype(
        jnp.bfloat16
    )
    merged = [
        merge_tile(base_weights[number], left_factors[number], scaled_right[number])
        for number in range(base_weights.shape[0])
    ]
    return jnp.stack(merged)


def any_spec():
    return pl.BlockSpec(memory_space=pl.ANY)


def vmem_spec():
    return pl.BlockSpec(memory_space=pltpu.VMEM)


def smem_spec():
    return pl.BlockSpec(memory_space=pltpu.SMEM)


def hop(value, move):
    col_count = lax.axis_size("col")
    row_count = lax.axis_size("row")
    ratio = row_count // col_count
    pairs = []
    for row in range(row_count):
        for plane in range(col_count):
            target = move(row // ratio, row % ratio, plane)
            if target is None or not 0 <= target[2] < col_count:
                continue
            pairs.append(
                (row * col_count + plane, (target[0] * ratio + target[1]) * col_count + target[2])
            )
    return lax.ppermute(value, ("row", "col"), pairs)


def chip_of():
    return lax.axis_index("row") // (lax.axis_size("row") // lax.axis_size("col"))


def scale_pieces(right, ranks, counts, slots, chips):
    proj, _, cap, width = right.shape
    sub = width // chips
    workers = ranks.shape[0]

    def kernel(ranks_ref, counts_ref, slots_ref, right_ref, *out_refs):
        plane = lax.axis_index("col")
        chip = chip_of()
        total = jnp.int32(0)
        own_rank = jnp.int32(0)
        own_count = jnp.int32(0)
        for w in range(workers):
            mine = slots_ref[w] == plane
            total = total + counts_ref[w]
            own_rank = own_rank + jnp.where(mine, ranks_ref[w], 0)
            own_count = own_count + jnp.where(mine, counts_ref[w], 0)
        tile = (8, LANES)
        total_f = jnp.full(tile, total, jnp.int32).astype(jnp.float32)
        count_f = jnp.full(tile, own_count, jnp.int32).astype(jnp.float32)
        rank_f = jnp.full(tile, own_rank, jnp.int32).astype(jnp.float32)
        scale = ADAPTER_ALPHA * (count_f / total_f) / rank_f
        scale_row = jnp.tile(scale[:1, :], (1, sub // LANES))
        for n in range(proj):
            for j in range(chips):
                start = pl.multiple_of((chip ^ j) * sub, LANES)
                block = right_ref[n, 0, :, pl.ds(start, sub)].astype(jnp.float32)
                out_refs[j][n] = (block * scale_row).astype(jnp.bfloat16)

    return pl.pallas_call(
        kernel,
        out_shape=[jax.ShapeDtypeStruct((proj, cap, sub), jnp.bfloat16)] * chips,
        in_specs=[smem_spec(), smem_spec(), smem_spec(), vmem_spec()],
        out_specs=[vmem_spec()] * chips,
        name="scale_pieces",
    )(ranks, counts, slots, right)


def by_distance(pieces, planes):
    count = 2 * planes - 1
    shape = pieces[0].shape

    def kernel(*refs):
        ins, outs = refs[:planes], refs[planes:]
        plane = lax.axis_index("col")
        chip = chip_of()
        for j in range(planes):
            distance = (chip ^ j) - plane + planes - 1
            for d in range(count):

                @pl.when(distance == d)
                def _():
                    outs[d][...] = ins[j][...]

    return pl.pallas_call(
        kernel,
        out_shape=[jax.ShapeDtypeStruct(shape, jnp.bfloat16)] * count,
        in_specs=[vmem_spec()] * planes,
        out_specs=[vmem_spec()] * count,
        name="by_distance",
    )(*pieces)


def slot_ranks(ranks_ref, slots_ref, workers):
    out = []
    for s in range(workers):
        rank = jnp.int32(0)
        for w in range(workers):
            rank = rank + jnp.where(slots_ref[w] == s, ranks_ref[w], 0)
        out.append(rank)
    return out


def pack_rows(parts, ranks, slots, total):
    planes = ranks.shape[0]
    count = len(parts)
    proj, cap, sub = parts[0].shape
    chunks = total // RANK_STEP

    def kernel(ranks_ref, slots_ref, *refs):
        ins, outs = refs[:count], refs[count:]
        plane = lax.axis_index("col")
        rank = slot_ranks(ranks_ref, slots_ref, planes)
        begin = jnp.int32(0)
        for s in range(planes):
            for d in range(planes - 1 - s, count - s):

                @pl.when(plane - s + planes - 1 == d)
                def _():
                    def step(g, carry):
                        source = pl.multiple_of(g * RANK_STEP, RANK_STEP)
                        target = pl.multiple_of(begin + g * RANK_STEP, RANK_STEP)
                        for n in range(proj):
                            outs[n][pl.ds(target, RANK_STEP), :] = ins[d][
                                n, pl.ds(source, RANK_STEP), :
                            ]
                        return carry

                    lax.fori_loop(0, rank[s] // RANK_STEP, step, 0)

            begin = begin + rank[s]

    return pl.pallas_call(
        kernel,
        out_shape=[jax.ShapeDtypeStruct((total, sub), jnp.bfloat16)] * proj,
        in_specs=[smem_spec(), smem_spec()] + [vmem_spec()] * count,
        out_specs=[vmem_spec()] * proj,
        name="pack_rows",
    )(ranks, slots, *parts)


def pack_left(parts, ranks, slots, total):
    planes = ranks.shape[0]
    count = len(parts)
    proj, rows, cap = parts[0].shape

    def kernel(ranks_ref, slots_ref, *refs):
        ins, out, buf = refs[:count], refs[count], refs[count + 1]
        plane = lax.axis_index("col")
        for s in range(planes):
            for d in range(planes - 1 - s, count - s):

                @pl.when(plane - s + planes - 1 == d)
                def _():
                    buf[s] = ins[d][...]

        rank = slot_ranks(ranks_ref, slots_ref, planes)
        begin = jnp.int32(0)
        picks = []
        for s in range(planes):
            source = lax.broadcasted_iota(jnp.int32, (cap, total), 0)
            target = lax.broadcasted_iota(jnp.int32, (cap, total), 1)
            picks.append(
                jnp.where((target - begin == source) & (source < rank[s]), 1.0, 0.0).astype(
                    jnp.bfloat16
                )
            )
            begin = begin + rank[s]
        for n in range(proj):
            acc = jnp.zeros((rows, total), jnp.float32)
            for s in range(planes):
                acc += jnp.dot(buf[s, n], picks[s], preferred_element_type=jnp.float32)
            out[n] = acc.astype(jnp.bfloat16)

    return pl.pallas_call(
        kernel,
        out_shape=jax.ShapeDtypeStruct((proj, rows, total), jnp.bfloat16),
        in_specs=[smem_spec(), smem_spec()] + [vmem_spec()] * count,
        out_specs=vmem_spec(),
        scratch_shapes=[pltpu.VMEM((planes, proj, rows, cap), jnp.bfloat16)],
        name="pack_left",
    )(ranks, slots, *parts)


def merge(number, base, left_pack, pieces, previous, chips, ratio):
    proj, rows, width = base.shape
    total, sub = pieces[0][0].shape
    count = ratio * chips
    group = 2 if chips % 2 == 0 else 1
    block = group * sub
    steps = width // block
    half_rows = 256

    def kernel(*refs):
        base_ref, left_ref = refs[0], refs[1]
        piece_refs = refs[2 : 2 + count]
        out_ref, right_buf, sem = refs[-3], refs[-2], refs[-1]
        chip = chip_of()
        core = lax.axis_index("row") % ratio
        step = pl.program_id(0)

        @pl.when(step == 0)
        def _():
            for k in range(ratio):
                for j in range(chips):
                    place = (core ^ k) * chips + (chip ^ j)
                    pltpu.make_async_copy(
                        piece_refs[k * chips + j], right_buf.at[place // group, place % group], sem.at[place]
                    ).start()

        for g in range(group):
            place = step * group + g
            pltpu.make_async_copy(piece_refs[0], right_buf.at[step, g], sem.at[place]).wait()
        for g in range(group):
            cols = pl.ds(g * sub, sub)
            for r in range(rows // half_rows):
                part = pl.ds(r * half_rows, half_rows)
                delta = jnp.dot(
                    left_ref[0, part, :], right_buf[step, g], preferred_element_type=jnp.float32
                )
                out_ref[0, part, cols] = (base_ref[0, part, cols].astype(jnp.float32) + delta).astype(
                    jnp.bfloat16
                )

    extra = [] if previous is None else [previous]
    return pl.pallas_call(
        kernel,
        out_shape=jax.ShapeDtypeStruct(base.shape, jnp.bfloat16),
        grid=(steps,),
        in_specs=[
            pl.BlockSpec((1, rows, block), lambda i: (number, 0, i)),
            pl.BlockSpec((1, rows, total), lambda i: (number, 0, 0)),
        ]
        + [any_spec()] * (count + len(extra)),
        out_specs=pl.BlockSpec((1, rows, block), lambda i: (number, 0, i)),
        scratch_shapes=[
            pltpu.VMEM((steps, group, total, sub), jnp.bfloat16),
            pltpu.SemaphoreType.DMA((count,)),
        ],
        input_output_aliases={2 + count: 0} if extra else {},
        name="merge",
    )(base, left_pack, *[piece for row in pieces for piece in row], *extra)


def exchange_planes(parts, planes):
    middle = planes - 1
    out = [None] * (2 * planes - 1)
    out[middle] = parts[middle]
    for distance in [2, 3, 1] if planes == 4 else range(1, planes):
        for sign in (1, -1):
            value = parts[middle + sign * distance]
            for done in range(distance):

                def move(chip, core, plane, done=done, distance=distance, sign=sign):
                    first = plane - sign * done
                    last = first + sign * distance
                    if not (0 <= first < planes and 0 <= last < planes):
                        return None
                    return (chip, core, plane + sign)

                value = hop(value, move)
            out[middle + sign * distance] = value
    return out


def spread_left(left, planes):
    middle = planes - 1
    out = [None] * (2 * planes - 1)
    out[middle] = left
    for sign in (1, -1):
        value = left
        for done in range(planes - 1):

            def move(chip, core, plane, done=done, sign=sign):
                if not 0 <= plane - sign * done < planes:
                    return None
                return (chip, core, plane + sign)

            value = hop(value, move)
            out[middle + sign * (done + 1)] = value
    return out


def fast_body(base_weights, left_factors, right_factors, client_adapter_ranks, step_counts, worker_slot):
    planes = lax.axis_size("col")
    ratio = lax.axis_size("row") // planes
    chips = planes
    proj = base_weights.shape[0]
    total = client_adapter_ranks.shape[0] * right_factors.shape[2] // 2
    left = left_factors.reshape(proj, -1, left_factors.shape[3])
    left_parts = spread_left(left, planes)
    own = scale_pieces(right_factors, client_adapter_ranks, step_counts, worker_slot, chips)
    near = [own[0]]
    for j in range(1, chips):
        near.append(hop(own[j], lambda chip, core, plane, j=j: (chip ^ j, core, plane)))
    parts = exchange_planes(by_distance(near, planes), planes)
    packs = pack_rows(parts, client_adapter_ranks, worker_slot, total)
    pieces = []
    for n in range(proj):
        packed = packs[n]
        first, second = (1, 2) if n % 2 == 0 else (2, 1)
        gathered = {0: packed}
        gathered[first] = hop(packed, lambda chip, core, plane: (chip ^ first, core, plane))
        gathered[second] = hop(packed, lambda chip, core, plane: (chip ^ second, core, plane))
        gathered[3] = hop(gathered[first], lambda chip, core, plane: (chip ^ second, core, plane))
        same = [gathered[j] for j in range(chips)]
        pieces.append(
            [same]
            + [
                [hop(v, lambda chip, core, plane, k=k: (chip, core ^ k, plane)) for v in same]
                for k in range(1, ratio)
            ]
        )
    left_pack = pack_left(left_parts, client_adapter_ranks, worker_slot, total)
    out = None
    for n in range(proj):
        out = merge(n, base_weights, left_pack, pieces[n], out, chips, ratio)
    return out


def solution(mesh):
    rows, cols = mesh.shape["row"], mesh.shape["col"]

    def body(base_weights, left_factors, right_factors, *rest):
        sub = right_factors.shape[3] // cols
        if rows == 2 * cols and cols == 4 and sub % LANES == 0:
            return fast_body(base_weights, left_factors, right_factors, *rest)
        return plain_body(base_weights, left_factors, right_factors, *rest)

    return jax.shard_map(
        body,
        mesh=mesh,
        in_specs=(
            P(None, "row", "col"),
            P(None, "row", "col", None),
            P(None, "col", None, "row"),
            P(),
            P(),
            P(),
        ),
        out_specs=P(None, "row", "col"),
        check_vma=False,
    )
```

```python
import jax
import jax.numpy as jnp
from jax import lax
from jax.experimental import pallas as pl
from jax.experimental.pallas import tpu as pltpu
from jax.sharding import PartitionSpec as P


ADAPTER_ALPHA = 32
LANES = 128
RANK_STEP = 16


def slot_tables(client_adapter_ranks, step_counts, worker_slot):
    workers = client_adapter_ranks.shape[0]
    slot_ids = jnp.arange(workers, dtype=jnp.int32)
    slot_hot = worker_slot[:, None] == slot_ids[None, :]
    rank_slot = jnp.sum(jnp.where(slot_hot, client_adapter_ranks[:, None], 0), axis=0)
    counts = step_counts.astype(jnp.float32)
    per_step_portion = counts / jnp.sum(counts)
    client_scale = ADAPTER_ALPHA * per_step_portion / client_adapter_ranks.astype(jnp.float32)
    slot_scale_factor = jnp.sum(jnp.where(slot_hot, client_scale[:, None], 0.0), axis=0)
    return (rank_slot, slot_scale_factor)


def merge_tile(base_tile, left_piece, right_piece):
    tile_rows = base_tile.shape[0]
    rank_cap = right_piece.shape[1]
    block_width = right_piece.shape[2]
    row_count = lax.axis_size("row")
    col_count = lax.axis_size("col")
    row_ratio = row_count // col_count
    left_all = lax.all_gather(left_piece, "col", axis=1, tiled=True)
    sub_width = block_width // row_count
    split_view = right_piece.reshape(1, rank_cap, row_count, sub_width)
    spread = lax.all_to_all(split_view, "row", split_axis=2, concat_axis=2, tiled=True)
    pair_view = spread.reshape(1, rank_cap, col_count, row_ratio, sub_width)
    slot_pieces = lax.all_to_all(pair_view, "col", split_axis=2, concat_axis=0, tiled=True)
    join_view = slot_pieces.reshape(col_count, rank_cap, row_ratio, 1, sub_width)
    joined = lax.all_gather(join_view, "row", axis=3, tiled=True)
    right_cols = joined.reshape(col_count, rank_cap, row_ratio * block_width)
    left_flat = left_all.reshape(tile_rows, -1)
    right_flat = right_cols.reshape(left_flat.shape[1], -1)
    delta_tile = jnp.dot(left_flat, right_flat, preferred_element_type=jnp.float32)
    return (base_tile.astype(jnp.float32) + delta_tile).astype(jnp.bfloat16)


def plain_body(base_weights, left_factors, right_factors, client_adapter_ranks, step_counts, worker_slot):
    workers = client_adapter_ranks.shape[0]
    rank_cap = right_factors.shape[2]
    rank_slot, slot_scale_factor = slot_tables(client_adapter_ranks, step_counts, worker_slot)
    own_hot = jnp.arange(workers, dtype=jnp.int32) == lax.axis_index("col")
    own_rank = jnp.sum(jnp.where(own_hot, rank_slot, 0))
    own_scale = jnp.sum(jnp.where(own_hot, slot_scale_factor, 0.0))
    rank_scale = jnp.where(jnp.arange(rank_cap, dtype=jnp.int32) < own_rank, own_scale, 0.0)
    scaled_right = (right_factors.astype(jnp.float32) * rank_scale[None, None, :, None]).astype(
        jnp.bfloat16
    )
    merged = [
        merge_tile(base_weights[number], left_factors[number], scaled_right[number])
        for number in range(base_weights.shape[0])
    ]
    return jnp.stack(merged)


def in_vmem(values):
    return [pltpu.with_memory_space_constraint(v, pltpu.VMEM) for v in values]


def vmem_out(shape):
    return pltpu.VMEM(shape, jnp.bfloat16)


def any_spec():
    return pl.BlockSpec(memory_space=pl.ANY)


def vmem_spec():
    return pl.BlockSpec(memory_space=pltpu.VMEM)


def smem_spec():
    return pl.BlockSpec(memory_space=pltpu.SMEM)


def hop(value, move):
    col_count = lax.axis_size("col")
    row_count = lax.axis_size("row")
    ratio = row_count // col_count
    pairs = []
    for row in range(row_count):
        for plane in range(col_count):
            target = move(row // ratio, row % ratio, plane)
            if target is None or not 0 <= target[2] < col_count:
                continue
            pairs.append(
                (row * col_count + plane, (target[0] * ratio + target[1]) * col_count + target[2])
            )
    return lax.ppermute(value, ("row", "col"), pairs)


def chip_of():
    return lax.axis_index("row") // (lax.axis_size("row") // lax.axis_size("col"))


def scale_pieces(number, right, ranks, counts, slots, chips):
    _, _, cap, width = right.shape
    sub = width // chips
    workers = ranks.shape[0]

    def kernel(ranks_ref, counts_ref, slots_ref, right_ref, *out_refs):
        plane = lax.axis_index("col")
        chip = chip_of()
        total = jnp.int32(0)
        own_rank = jnp.int32(0)
        own_count = jnp.int32(0)
        for w in range(workers):
            mine = slots_ref[w] == plane
            total = total + counts_ref[w]
            own_rank = own_rank + jnp.where(mine, ranks_ref[w], 0)
            own_count = own_count + jnp.where(mine, counts_ref[w], 0)
        tile = (8, LANES)
        total_f = jnp.full(tile, total, jnp.int32).astype(jnp.float32)
        count_f = jnp.full(tile, own_count, jnp.int32).astype(jnp.float32)
        rank_f = jnp.full(tile, own_rank, jnp.int32).astype(jnp.float32)
        scale = ADAPTER_ALPHA * (count_f / total_f) / rank_f
        scale_row = jnp.tile(scale[:1, :], (1, sub // LANES))
        for j in range(chips):
            start = pl.multiple_of((chip ^ j) * sub, LANES)
            block = right_ref[0, 0, :, pl.ds(start, sub)].astype(jnp.float32)
            out_refs[j][...] = (block * scale_row).astype(jnp.bfloat16)

    return pl.pallas_call(
        kernel,
        out_shape=[vmem_out((cap, sub))] * chips,
        grid=(1,),
        in_specs=[
            smem_spec(),
            smem_spec(),
            smem_spec(),
            pl.BlockSpec((1, 1, cap, width), lambda i: (number, 0, 0, 0)),
        ],
        out_specs=[vmem_spec()] * chips,
        name="scale_pieces",
    )(ranks, counts, slots, right)


def by_plane(pieces, planes):
    shape = pieces[0].shape

    def kernel(*refs):
        ins, outs = refs[:planes], refs[planes:]
        shift = lax.axis_index("col") ^ chip_of()
        for d in range(planes):

            @pl.when(shift == d)
            def _():
                for j in range(planes):
                    outs[j ^ d][...] = ins[j][...]

    return pl.pallas_call(
        kernel,
        out_shape=[vmem_out(shape)] * planes,
        in_specs=[vmem_spec()] * planes,
        out_specs=[vmem_spec()] * planes,
        compiler_params=pltpu.CompilerParams(vmem_limit_bytes=4 << 20),
        name="by_plane",
    )(*in_vmem(pieces))


def slot_ranks(ranks_ref, slots_ref, workers):
    out = []
    for s in range(workers):
        rank = jnp.int32(0)
        for w in range(workers):
            rank = rank + jnp.where(slots_ref[w] == s, ranks_ref[w], 0)
        out.append(rank)
    return out


def pack_rows(parts, ranks, slots, total):
    planes = ranks.shape[0]
    count = len(parts)
    _, sub = parts[0].shape

    def kernel(ranks_ref, slots_ref, *refs):
        ins, out = refs[:count], refs[count]
        plane = lax.axis_index("col")
        rank = slot_ranks(ranks_ref, slots_ref, planes)
        begin = jnp.int32(0)
        for s in range(planes):
            for d in range(planes):

                @pl.when(plane ^ s == d)
                def _():
                    def step(g, carry):
                        source = pl.multiple_of(g * RANK_STEP, RANK_STEP)
                        target = pl.multiple_of(begin + g * RANK_STEP, RANK_STEP)
                        out[pl.ds(target, RANK_STEP), :] = ins[d][pl.ds(source, RANK_STEP), :]
                        return carry

                    lax.fori_loop(0, rank[s] // RANK_STEP, step, 0)

            begin = begin + rank[s]

    return pl.pallas_call(
        kernel,
        out_shape=vmem_out((total, sub)),
        in_specs=[smem_spec(), smem_spec()] + [vmem_spec()] * count,
        out_specs=vmem_spec(),
        compiler_params=pltpu.CompilerParams(vmem_limit_bytes=4 << 20),
        name="pack_rows",
    )(ranks, slots, *in_vmem(parts))


def pack_left(parts, ranks, slots, total):
    planes = ranks.shape[0]
    count = len(parts)
    rows, cap = parts[0].shape

    def kernel(ranks_ref, slots_ref, *refs):
        ins, out, buf = refs[:count], refs[count], refs[count + 1]
        plane = lax.axis_index("col")
        for s in range(planes):
            for d in range(planes):

                @pl.when(plane ^ s == d)
                def _():
                    buf[s] = ins[d][...]

        rank = slot_ranks(ranks_ref, slots_ref, planes)
        begin = jnp.int32(0)
        picks = []
        for s in range(planes):
            source = lax.broadcasted_iota(jnp.int32, (cap, total), 0)
            target = lax.broadcasted_iota(jnp.int32, (cap, total), 1)
            picks.append(
                jnp.where((target - begin == source) & (source < rank[s]), 1.0, 0.0).astype(
                    jnp.bfloat16
                )
            )
            begin = begin + rank[s]
        acc = jnp.zeros((rows, total), jnp.float32)
        for s in range(planes):
            acc += jnp.dot(buf[s], picks[s], preferred_element_type=jnp.float32)
        out[...] = acc.astype(jnp.bfloat16)

    return pl.pallas_call(
        kernel,
        out_shape=jax.ShapeDtypeStruct((rows, total), jnp.bfloat16),
        in_specs=[smem_spec(), smem_spec()] + [vmem_spec()] * count,
        out_specs=vmem_spec(),
        scratch_shapes=[pltpu.VMEM((planes, rows, cap), jnp.bfloat16)],
        compiler_params=pltpu.CompilerParams(vmem_limit_bytes=16 << 20),
        name="pack_left",
    )(ranks, slots, *in_vmem(parts))


def load_base(number, base):
    _, rows, width = base.shape
    parts = 4

    def kernel(base_ref, out_ref, sem):
        copies = []
        for i in range(parts):
            part = pl.ds(i * (rows // parts), rows // parts)
            copies.append(
                pltpu.make_async_copy(base_ref.at[number, part], out_ref.at[part], sem.at[i])
            )
        for copy in copies:
            copy.start()
        for copy in copies:
            copy.wait()

    return pl.pallas_call(
        kernel,
        out_shape=vmem_out((rows, width)),
        in_specs=[any_spec()],
        out_specs=vmem_spec(),
        scratch_shapes=[pltpu.SemaphoreType.DMA((parts,))],
        compiler_params=pltpu.CompilerParams(vmem_limit_bytes=2 << 20),
        name="load_base",
    )(base)


def merge(number, proj, base, left_pack, pieces, previous, chips, ratio):
    rows, width = base.shape
    total, sub = pieces[0][0].shape
    count = ratio * chips
    group = 2 if chips % 2 == 0 else 1
    block = group * sub
    steps = width // block
    part_rows = 256

    def kernel(*refs):
        base_ref, left_ref = refs[0], refs[1]
        piece_refs = refs[2 : 2 + count]
        out_ref, right_buf, sem = refs[-3], refs[-2], refs[-1]
        chip = chip_of()
        core = lax.axis_index("row") % ratio
        step = pl.program_id(0)

        @pl.when(step == 0)
        def _():
            for k in range(ratio):
                for j in range(chips):
                    place = (core ^ k) * chips + (chip ^ j)
                    lanes = pl.ds(pl.multiple_of(place % group * sub, LANES), sub)
                    pltpu.make_async_copy(
                        piece_refs[k * chips + j], right_buf.at[place // group, :, lanes], sem.at[place]
                    ).start()

        for g in range(group):
            lanes = pl.ds(g * sub, sub)
            pltpu.make_async_copy(
                piece_refs[0], right_buf.at[step, :, lanes], sem.at[step * group + g]
            ).wait()
        source = pl.ds(pl.multiple_of(step * block, LANES), block)
        for r in range(rows // part_rows):
            part = pl.ds(r * part_rows, part_rows)
            delta = jnp.dot(left_ref[part, :], right_buf[step], preferred_element_type=jnp.float32)
            out_ref[0, part, :] = (base_ref[part, source].astype(jnp.float32) + delta).astype(
                jnp.bfloat16
            )

    extra = [] if previous is None else [previous]
    return pl.pallas_call(
        kernel,
        out_shape=jax.ShapeDtypeStruct((proj, rows, width), jnp.bfloat16),
        grid=(steps,),
        in_specs=[
            vmem_spec(),
            pl.BlockSpec((rows, total), lambda i: (0, 0)),
        ]
        + [any_spec()] * (count + len(extra)),
        out_specs=pl.BlockSpec((1, rows, block), lambda i: (number, 0, i)),
        scratch_shapes=[
            pltpu.VMEM((steps, total, block), jnp.bfloat16),
            pltpu.SemaphoreType.DMA((count,)),
        ],
        input_output_aliases={2 + count: 0} if extra else {},
        compiler_params=pltpu.CompilerParams(vmem_limit_bytes=16 << 20),
        name="merge",
    )(base, left_pack, *[piece for row in pieces for piece in row], *extra)


def swap_planes(parts):
    out = list(parts)
    for i in range(len(parts) - 1, 0, -1):
        out[i] = hop(parts[i], lambda chip, core, plane: (chip, core, plane ^ i))
    return out


def spread_left(left, planes):
    out = [left]
    for i in range(1, planes):
        low = i & (i - 1)
        if low:
            source, step = out[low], i ^ low
        else:
            source, step = left, i
        out.append(hop(source, lambda chip, core, plane: (chip, core, plane ^ step)))
    return out


def fast_body(base_weights, left_factors, right_factors, client_adapter_ranks, step_counts, worker_slot):
    planes = lax.axis_size("col")
    ratio = lax.axis_size("row") // planes
    chips = planes
    proj = base_weights.shape[0]
    total = client_adapter_ranks.shape[0] * right_factors.shape[2] // 2
    left = [left_factors[n, :, 0, :] for n in range(proj)]
    pieces = []
    for n in range(proj):
        near = []
        own = scale_pieces(n, right_factors, client_adapter_ranks, step_counts, worker_slot, chips)
        for j in range(chips):
            piece = own[j]
            if j:
                piece = hop(piece, lambda chip, core, plane: (chip ^ j, core, plane))
            near.append(piece)
        parts = by_plane(near, planes)
        parts = swap_planes(parts)
        packed = pack_rows(parts, client_adapter_ranks, worker_slot, total)
        same = [packed]
        for j in range(1, chips):
            relay = n == 0 and j == 3
            step = j ^ 1 if relay else j
            same.append(
                hop(
                    same[1] if relay else packed,
                    lambda chip, core, plane: (chip ^ step, core, plane),
                )
            )
        pieces.append(
            [same]
            + [
                [hop(v, lambda chip, core, plane: (chip, core ^ k, plane)) for v in same]
                for k in range(1, ratio)
            ]
        )
    base = []
    for n in range(proj):
        base.append(load_base(n, pltpu.with_memory_space_constraint(base_weights, pltpu.HBM)))
    out = None
    for n in range(proj):
        left_parts = spread_left(left[n], planes)
        left_pack = pack_left(left_parts, client_adapter_ranks, worker_slot, total)
        out = merge(n, proj, base[n], left_pack, pieces[n], out, chips, ratio)
    return out


def solution(mesh):
    rows, cols = mesh.shape["row"], mesh.shape["col"]

    def body(base_weights, left_factors, right_factors, *rest):
        sub = right_factors.shape[3] // cols
        fast = rows == 2 * cols and cols == 4 and sub % LANES == 0
        if not fast:
            return plain_body(base_weights, left_factors, right_factors, *rest)
        return fast_body(base_weights, left_factors, right_factors, *rest)

    return jax.shard_map(
        body,
        mesh=mesh,
        in_specs=(
            P(None, "row", "col"),
            P(None, "row", "col", None),
            P(None, "col", None, "row"),
            P(),
            P(),
            P(),
        ),
        out_specs=P(None, "row", "col"),
        check_vma=False,
    )
```

```python
import jax
import jax.numpy as jnp
from jax import lax
from jax.experimental import pallas as pl
from jax.experimental.pallas import tpu as pltpu
from jax.sharding import PartitionSpec as P


ADAPTER_ALPHA = 32
LANES = 128
RANK_STEP = 16
FIRST_BANDS = 2


def slot_tables(client_adapter_ranks, step_counts, worker_slot):
    workers = client_adapter_ranks.shape[0]
    slot_ids = jnp.arange(workers, dtype=jnp.int32)
    slot_hot = worker_slot[:, None] == slot_ids[None, :]
    rank_slot = jnp.sum(jnp.where(slot_hot, client_adapter_ranks[:, None], 0), axis=0)
    counts = step_counts.astype(jnp.float32)
    per_step_portion = counts / jnp.sum(counts)
    client_scale = ADAPTER_ALPHA * per_step_portion / client_adapter_ranks.astype(jnp.float32)
    slot_scale_factor = jnp.sum(jnp.where(slot_hot, client_scale[:, None], 0.0), axis=0)
    return (rank_slot, slot_scale_factor)


def merge_tile(base_tile, left_piece, right_piece):
    tile_rows = base_tile.shape[0]
    rank_cap = right_piece.shape[1]
    block_width = right_piece.shape[2]
    row_count = lax.axis_size("row")
    col_count = lax.axis_size("col")
    row_ratio = row_count // col_count
    left_all = lax.all_gather(left_piece, "col", axis=1, tiled=True)
    sub_width = block_width // row_count
    split_view = right_piece.reshape(1, rank_cap, row_count, sub_width)
    spread = lax.all_to_all(split_view, "row", split_axis=2, concat_axis=2, tiled=True)
    pair_view = spread.reshape(1, rank_cap, col_count, row_ratio, sub_width)
    slot_pieces = lax.all_to_all(pair_view, "col", split_axis=2, concat_axis=0, tiled=True)
    join_view = slot_pieces.reshape(col_count, rank_cap, row_ratio, 1, sub_width)
    joined = lax.all_gather(join_view, "row", axis=3, tiled=True)
    right_cols = joined.reshape(col_count, rank_cap, row_ratio * block_width)
    left_flat = left_all.reshape(tile_rows, -1)
    right_flat = right_cols.reshape(left_flat.shape[1], -1)
    delta_tile = jnp.dot(left_flat, right_flat, preferred_element_type=jnp.float32)
    return (base_tile.astype(jnp.float32) + delta_tile).astype(jnp.bfloat16)


def plain_body(base_weights, left_factors, right_factors, client_adapter_ranks, step_counts, worker_slot):
    workers = client_adapter_ranks.shape[0]
    rank_cap = right_factors.shape[2]
    rank_slot, slot_scale_factor = slot_tables(client_adapter_ranks, step_counts, worker_slot)
    own_hot = jnp.arange(workers, dtype=jnp.int32) == lax.axis_index("col")
    own_rank = jnp.sum(jnp.where(own_hot, rank_slot, 0))
    own_scale = jnp.sum(jnp.where(own_hot, slot_scale_factor, 0.0))
    rank_scale = jnp.where(jnp.arange(rank_cap, dtype=jnp.int32) < own_rank, own_scale, 0.0)
    scaled_right = (right_factors.astype(jnp.float32) * rank_scale[None, None, :, None]).astype(
        jnp.bfloat16
    )
    merged = [
        merge_tile(base_weights[number], left_factors[number], scaled_right[number])
        for number in range(base_weights.shape[0])
    ]
    return jnp.stack(merged)


def in_vmem(values):
    return [pltpu.with_memory_space_constraint(v, pltpu.VMEM) for v in values]


def vmem_out(shape):
    return pltpu.VMEM(shape, jnp.bfloat16)


def any_spec():
    return pl.BlockSpec(memory_space=pl.ANY)


def vmem_spec():
    return pl.BlockSpec(memory_space=pltpu.VMEM)


def smem_spec():
    return pl.BlockSpec(memory_space=pltpu.SMEM)


def hop(value, move):
    col_count = lax.axis_size("col")
    row_count = lax.axis_size("row")
    ratio = row_count // col_count
    pairs = []
    for row in range(row_count):
        for plane in range(col_count):
            target = move(row // ratio, row % ratio, plane)
            if target is None or not 0 <= target[2] < col_count:
                continue
            pairs.append(
                (row * col_count + plane, (target[0] * ratio + target[1]) * col_count + target[2])
            )
    return lax.ppermute(value, ("row", "col"), pairs)


def chip_of():
    return lax.axis_index("row") // (lax.axis_size("row") // lax.axis_size("col"))


def scale_pieces(number, right, left, ranks, counts, slots, chips, bands):
    _, _, cap, width = right.shape
    _, rows, _ = left.shape
    band = cap // bands
    sub = width // chips
    workers = ranks.shape[0]

    def kernel(ranks_ref, counts_ref, slots_ref, right_ref, left_ref, *out_refs):
        plane = lax.axis_index("col")
        chip = chip_of()
        total = jnp.int32(0)
        own_rank = jnp.int32(0)
        own_count = jnp.int32(0)
        for w in range(workers):
            mine = slots_ref[w] == plane
            total = total + counts_ref[w]
            own_rank = own_rank + jnp.where(mine, ranks_ref[w], 0)
            own_count = own_count + jnp.where(mine, counts_ref[w], 0)
        tile = (8, LANES)
        total_f = jnp.full(tile, total, jnp.int32).astype(jnp.float32)
        count_f = jnp.full(tile, own_count, jnp.int32).astype(jnp.float32)
        rank_f = jnp.full(tile, own_rank, jnp.int32).astype(jnp.float32)
        scale = ADAPTER_ALPHA * (count_f / total_f) / rank_f
        scale_row = jnp.tile(scale[:1, :], (1, sub // LANES))
        out_refs[bands * chips][...] = left_ref[0]
        for h in range(bands):
            for j in range(chips):
                start = pl.multiple_of((chip ^ j) * sub, LANES)
                block = right_ref[0, 0, pl.ds(h * band, band), pl.ds(start, sub)]
                out_refs[h * chips + j][...] = (block.astype(jnp.float32) * scale_row).astype(
                    jnp.bfloat16
                )

    return pl.pallas_call(
        kernel,
        out_shape=[vmem_out((band, sub))] * (bands * chips) + [vmem_out((rows, cap))],
        grid=(1,),
        in_specs=[
            smem_spec(),
            smem_spec(),
            smem_spec(),
            pl.BlockSpec((1, 1, cap, width), lambda i: (number, 0, 0, 0)),
            pl.BlockSpec((1, rows, cap), lambda i: (number, 0, 0)),
        ],
        out_specs=[vmem_spec()] * (bands * chips + 1),
        name="scale_pieces",
    )(ranks, counts, slots, right, left)


def by_plane(pieces, planes):
    shape = pieces[0].shape

    def kernel(*refs):
        ins, outs = refs[:planes], refs[planes:]
        shift = lax.axis_index("col") ^ chip_of()
        for d in range(planes):

            @pl.when(shift == d)
            def _():
                for j in range(planes):
                    outs[j ^ d][...] = ins[j][...]

    return pl.pallas_call(
        kernel,
        out_shape=[vmem_out(shape)] * planes,
        in_specs=[vmem_spec()] * planes,
        out_specs=[vmem_spec()] * planes,
        compiler_params=pltpu.CompilerParams(vmem_limit_bytes=4 << 20),
        name="by_plane",
    )(*in_vmem(pieces))


def slot_ranks(ranks_ref, slots_ref, workers):
    out = []
    for s in range(workers):
        rank = jnp.int32(0)
        for w in range(workers):
            rank = rank + jnp.where(slots_ref[w] == s, ranks_ref[w], 0)
        out.append(rank)
    return out


def pack_rows(bands, ranks, slots, total):
    planes = ranks.shape[0]
    band, sub = bands[0][0].shape

    def kernel(ranks_ref, slots_ref, *refs):
        ins, out = refs[:-1], refs[-1]
        plane = lax.axis_index("col")
        rank = slot_ranks(ranks_ref, slots_ref, planes)
        begin = jnp.int32(0)
        for s in range(planes):
            for d in range(planes):

                @pl.when(plane ^ s == d)
                def _():
                    for h in range(len(bands)):

                        def step(g, carry):
                            source = pl.multiple_of(g * RANK_STEP, RANK_STEP)
                            target = pl.multiple_of(begin + h * band + g * RANK_STEP, RANK_STEP)
                            out[pl.ds(target, RANK_STEP), :] = ins[h * planes + d][
                                pl.ds(source, RANK_STEP), :
                            ]
                            return carry

                        valid = jnp.clip(rank[s] - h * band, 0, band)
                        lax.fori_loop(0, valid // RANK_STEP, step, 0)

            begin = begin + rank[s]

    parts = [part for parts in bands for part in parts]
    return pl.pallas_call(
        kernel,
        out_shape=vmem_out((total, sub)),
        in_specs=[smem_spec(), smem_spec()] + [vmem_spec()] * len(parts),
        out_specs=vmem_spec(),
        compiler_params=pltpu.CompilerParams(vmem_limit_bytes=4 << 20),
        name="pack_rows",
    )(ranks, slots, *in_vmem(parts))


def pack_left(parts, ranks, slots, total):
    planes = ranks.shape[0]
    count = len(parts)
    rows, cap = parts[0].shape

    def kernel(ranks_ref, slots_ref, *refs):
        ins, out, buf = refs[:count], refs[count], refs[count + 1]
        plane = lax.axis_index("col")
        for s in range(planes):
            for d in range(planes):

                @pl.when(plane ^ s == d)
                def _():
                    buf[s] = ins[d][...]

        rank = slot_ranks(ranks_ref, slots_ref, planes)
        begin = jnp.int32(0)
        picks = []
        for s in range(planes):
            source = lax.broadcasted_iota(jnp.int32, (cap, total), 0)
            target = lax.broadcasted_iota(jnp.int32, (cap, total), 1)
            picks.append(
                jnp.where((target - begin == source) & (source < rank[s]), 1.0, 0.0).astype(
                    jnp.bfloat16
                )
            )
            begin = begin + rank[s]
        acc = jnp.zeros((rows, total), jnp.float32)
        for s in range(planes):
            acc += jnp.dot(buf[s], picks[s], preferred_element_type=jnp.float32)
        out[...] = acc.astype(jnp.bfloat16)

    return pl.pallas_call(
        kernel,
        out_shape=jax.ShapeDtypeStruct((rows, total), jnp.bfloat16),
        in_specs=[smem_spec(), smem_spec()] + [vmem_spec()] * count,
        out_specs=vmem_spec(),
        scratch_shapes=[pltpu.VMEM((planes, rows, cap), jnp.bfloat16)],
        compiler_params=pltpu.CompilerParams(vmem_limit_bytes=16 << 20),
        name="pack_left",
    )(ranks, slots, *in_vmem(parts))


def load_base(number, base):
    _, rows, width = base.shape
    parts = 4

    def kernel(base_ref, out_ref, sem):
        copies = []
        for i in range(parts):
            part = pl.ds(i * (rows // parts), rows // parts)
            copies.append(
                pltpu.make_async_copy(base_ref.at[number, part], out_ref.at[part], sem.at[i])
            )
        for copy in copies:
            copy.start()
        for copy in copies:
            copy.wait()

    return pl.pallas_call(
        kernel,
        out_shape=vmem_out((rows, width)),
        in_specs=[any_spec()],
        out_specs=vmem_spec(),
        scratch_shapes=[pltpu.SemaphoreType.DMA((parts,))],
        compiler_params=pltpu.CompilerParams(vmem_limit_bytes=2 << 20),
        name="load_base",
    )(base)


def merge(number, proj, base, left_pack, pieces, previous, chips, ratio):
    rows, width = base.shape
    total, sub = pieces[0][0].shape
    bands = [part for parts in pieces for part in parts]
    count = ratio * chips
    group = 2 if chips % 2 == 0 else 1
    block = group * sub
    steps = width // block
    part_rows = 256

    def kernel(*refs):
        base_ref, left_ref = refs[0], refs[1]
        piece_refs = iter(refs[2 : 2 + len(bands)])
        whole = refs[2]
        out_ref, right_buf, sem = refs[-3], refs[-2], refs[-1]
        chip = chip_of()
        core = lax.axis_index("row") % ratio
        step = pl.program_id(0)

        @pl.when(step == 0)
        def _():
            for k in range(ratio):
                for j in range(chips):
                    place = (core ^ k) * chips + (chip ^ j)
                    lanes = pl.ds(pl.multiple_of(place % group * sub, LANES), sub)
                    top = 0
                    for part in pieces[k * chips + j]:
                        band = pl.ds(top, part.shape[0])
                        pltpu.make_async_copy(
                            next(piece_refs), right_buf.at[place // group, band, lanes], sem.at[place]
                        ).start()
                        top += part.shape[0]

        for g in range(group):
            lanes = pl.ds(g * sub, sub)
            pltpu.make_async_copy(
                whole, right_buf.at[step, :, lanes], sem.at[step * group + g]
            ).wait()
        source = pl.ds(pl.multiple_of(step * block, LANES), block)
        for r in range(rows // part_rows):
            part = pl.ds(r * part_rows, part_rows)
            delta = jnp.dot(left_ref[part, :], right_buf[step], preferred_element_type=jnp.float32)
            out_ref[0, part, :] = (base_ref[part, source].astype(jnp.float32) + delta).astype(
                jnp.bfloat16
            )

    extra = [] if previous is None else [previous]
    return pl.pallas_call(
        kernel,
        out_shape=jax.ShapeDtypeStruct((proj, rows, width), jnp.bfloat16),
        grid=(steps,),
        in_specs=[
            vmem_spec(),
            pl.BlockSpec((rows, total), lambda i: (0, 0)),
        ]
        + [any_spec()] * (len(bands) + len(extra)),
        out_specs=pl.BlockSpec((1, rows, block), lambda i: (number, 0, i)),
        scratch_shapes=[
            pltpu.VMEM((steps, total, block), jnp.bfloat16),
            pltpu.SemaphoreType.DMA((count,)),
        ],
        input_output_aliases={2 + len(bands): 0} if extra else {},
        compiler_params=pltpu.CompilerParams(vmem_limit_bytes=16 << 20),
        name="merge",
    )(base, left_pack, *bands, *extra)


def swap_planes(parts):
    out = list(parts)
    for i in range(len(parts) - 1, 0, -1):
        out[i] = hop(parts[i], lambda chip, core, plane: (chip, core, plane ^ i))
    return out


def spread_left(left, planes):
    out = [left]
    for i in range(1, planes):
        low = i & (i - 1)
        if low:
            source, step = out[low], i ^ low
        else:
            source, step = left, i
        out.append(hop(source, lambda chip, core, plane: (chip, core, plane ^ step)))
    return out


def fast_body(base_weights, left_factors, right_factors, client_adapter_ranks, step_counts, worker_slot):
    planes = lax.axis_size("col")
    ratio = lax.axis_size("row") // planes
    chips = planes
    proj = base_weights.shape[0]
    total = client_adapter_ranks.shape[0] * right_factors.shape[2] // 2
    left_flat = left_factors.reshape(proj, -1, left_factors.shape[3])
    left = []
    pieces = []
    for n in range(proj):
        count = FIRST_BANDS if n == 0 else 1
        *own, left_own = scale_pieces(
            n,
            right_factors,
            left_flat,
            client_adapter_ranks,
            step_counts,
            worker_slot,
            chips,
            count,
        )
        left.append(left_own)
        bands = []
        for h in range(count):
            near = []
            for j in range(chips):
                piece = own[h * chips + j]
                if j:
                    piece = hop(piece, lambda chip, core, plane: (chip ^ j, core, plane))
                near.append(piece)
            parts = by_plane(near, planes)
            bands.append(swap_planes(parts))
        packed = pack_rows(bands, client_adapter_ranks, worker_slot, total)
        near_x = hop(packed, lambda chip, core, plane: (chip ^ 1, core, plane))
        near_y = hop(packed, lambda chip, core, plane: (chip ^ 2, core, plane))
        half = total // 2
        diagonal = [
            hop(near_x[:half], lambda chip, core, plane: (chip ^ 2, core, plane)),
            hop(near_y[half:], lambda chip, core, plane: (chip ^ 1, core, plane)),
        ]
        same = [[packed], [near_x], [near_y], diagonal]
        pieces.append(same)
        for k in range(1, ratio):
            pieces[n] = pieces[n] + [
                [hop(part, lambda chip, core, plane: (chip, core ^ k, plane)) for part in parts]
                for parts in same
            ]
    base = []
    for n in range(proj):
        base.append(load_base(n, pltpu.with_memory_space_constraint(base_weights, pltpu.HBM)))
    out = None
    for n in range(proj):
        left_parts = spread_left(left[n], planes)
        left_pack = pack_left(left_parts, client_adapter_ranks, worker_slot, total)
        out = merge(n, proj, base[n], left_pack, pieces[n], out, chips, ratio)
    return out


def solution(mesh):
    rows, cols = mesh.shape["row"], mesh.shape["col"]

    def body(base_weights, left_factors, right_factors, *rest):
        sub = right_factors.shape[3] // cols
        fast = rows == 2 * cols and cols == 4 and sub % LANES == 0
        if not fast:
            return plain_body(base_weights, left_factors, right_factors, *rest)
        return fast_body(base_weights, left_factors, right_factors, *rest)

    return jax.shard_map(
        body,
        mesh=mesh,
        in_specs=(
            P(None, "row", "col"),
            P(None, "row", "col", None),
            P(None, "col", None, "row"),
            P(),
            P(),
            P(),
        ),
        out_specs=P(None, "row", "col"),
        check_vma=False,
    )
```
